32 devices in a mesh: tm: 16 (over z, y, core), space: 2 (over x).
Axes of the slice: x: 2, y: 2, z: 4, core: 2. Of those that a mesh axis runs over, the one named last changes fastest.
Arguments:
- cpoint_guess: float32 [16, 3, 32, 1024], P('tm', None, 'space'), may hold values from -6 to 6
- tide_forcing: float32 [128, 3, 32, 1024], P('tm', None, 'space'), may hold values from -4 to 4
- depth: float32 [32, 1024], P('space'), may hold values from 0.5 to 1.5
- drag: float32 [32, 1024], P('space'), may hold values from 0.01 to 0.08
Outputs:
- improved: float32 [128, 3, 32, 1024], P('tm', None, 'space')
- cpoint_residual: float32 [16, 3, 32, 1024], P('tm', None, 'space')
The draws below stay inside these ranges and needn't reach their ends.
All inputs are finite; a program needn't handle non-finite values.
Results may differ from the reference program's by a relative error of at most 0.0003.
Values sent between devices are 32-bit elements; how exact they have to be, the bound alone decides.
A program may use at most 128 MiB of HBM per device.

```python
import math
import jax
import jax.numpy as jnp

NY = 1024
T_DEV = 8
LEVELS = 5
NX = 32
TIMES = 128
N_TM = 16


def block_scale(key, extent, split, low, high):
    gain = 1.0
    for position, parts in split:
        draws = jax.random.uniform(jax.random.fold_in(jax.random.fold_in(key, 6), position), (parts,), jnp.float32, low / len(split), high / len(split))
        gain = gain * jnp.repeat(jnp.exp(draws), extent[position] // parts).reshape((-1,) + (1,) * (len(extent) - 1 - position))
    return gain


def centred(key, shape, spread, most, split=(), held_as=jnp.bfloat16):
    gain = block_scale(key, shape, split, -0.22, 0.18) if split else 1.0
    entries = jax.random.normal(key, shape, jnp.float32) * spread * gain
    return jnp.minimum(jnp.maximum(entries, -most), most).astype(held_as)


def setup_inputs(seed: int = 0) -> dict:
    key_list = jax.random.split(jax.random.key(seed), 5)
    cpoint_guess = centred(key_list[0], (N_TM, 3, NX, NY), 1.0, 6.0, ((0, 16), (2, 2)), jnp.float32)
    tide_forcing = centred(key_list[1], (TIMES, 3, NX, NY), 0.5, 4.0, ((0, 16), (2, 2)), jnp.float32)
    depth = jnp.clip(0.5 + 1.0 * jax.random.uniform(key_list[2], (NX, NY), jnp.float32) ** block_scale(key_list[2], (NX, NY), ((0, 2),), -0.2, 0.2), 0.5, 1.5)
    drag = jnp.clip(jnp.exp(math.log(0.08) - 2.0794415 * jax.random.uniform(key_list[3], (NX, NY), jnp.float32) ** block_scale(key_list[3], (NX, NY), ((0, 2),), -0.2, 0.2)), 0.01, 0.08)
    return {"cpoint_guess": cpoint_guess, "tide_forcing": tide_forcing, "depth": depth, "drag": drag}


coriolis = 0.1
fine_courant = 0.25
coarse_courant = 0.5


def along_rows(field):
    return (jnp.roll(field, -1, -2) - jnp.roll(field, 1, -2)) * 0.5


def along_cols(field):
    return (jnp.roll(field, -1, -1) - jnp.roll(field, 1, -1)) * 0.5


def substep(state, depth, drag, courant):
    height = state[..., 0, :, :]
    eastward = state[..., 1, :, :]
    northward = state[..., 2, :, :]
    new_height = height - courant * depth * (along_rows(eastward) + along_cols(northward))
    retain = 1.0 - drag
    new_east = retain * eastward + courant * coriolis * northward - courant * along_rows(new_height)
    new_north = retain * northward - courant * coriolis * eastward - courant * along_cols(new_height)
    return jnp.stack((new_height, new_east, new_north), axis=-3)


def reference(cpoint_guess, tide_forcing, depth, drag):
    forcing = tide_forcing.reshape(N_TM, T_DEV, 3, NX, NY)

    def fine(state):
        return substep(substep(state, depth, drag, fine_courant), depth, drag, fine_courant)

    def coarse(state):
        return substep(state, depth, drag, coarse_courant)

    state = cpoint_guess
    for moment in range(1, T_DEV):
        state = fine(state) + forcing[:, moment]
    right = jnp.roll(fine(state), 1, axis=0) + forcing[:, 0] - cpoint_guess
    rights = [right]
    for level in range(1, LEVELS):
        current = rights[-1]
        earlier = jnp.roll(current, 1, axis=0)[0::2]
        rights.append(current[0::2] + coarse(earlier))
    base = rights[-1]
    points = base.shape[0]
    correction = base
    for counter in range(1, points + 1):
        spot = counter % points
        correction = correction.at[spot].set(coarse(correction[(spot - 1) % points]) + base[spot])
    for level in range(LEVELS - 1, 0, -1):
        current = rights[level - 1]
        odd_points = coarse(correction) + current[1::2]
        correction = jnp.stack((correction, odd_points), axis=1).reshape(current.shape)
    state = cpoint_guess + correction
    states = [state]
    for moment in range(1, T_DEV):
        state = fine(state) + forcing[:, moment]
        states.append(state)
    improved = jnp.stack(states, axis=1).reshape(N_TM * T_DEV, 3, NX, NY)
    return improved, right
```

```python
import jax
import jax.numpy as jnp
from jax import lax
from jax.experimental import pallas as pl
from jax.experimental.pallas import tpu as pltpu
from jax.sharding import PartitionSpec as P

LEVELS = 5


coriolis = 0.1
fine_courant = 0.25
coarse_courant = 0.5


def with_halo(cells, sides, width):
    for axis, dim in sides:
        count = lax.axis_size(axis)
        head = lax.slice_in_dim(cells, 0, width, axis=dim)
        tail = lax.slice_in_dim(cells, cells.shape[dim] - width, cells.shape[dim], axis=dim)
        cells = jnp.concatenate(
            [
                lax.ppermute(tail, axis, [(i, (i + 1) % count) for i in range(count)]),
                cells,
                lax.ppermute(head, axis, [((i + 1) % count, i) for i in range(count)]),
            ],
            axis=dim,
        )
    return cells


def shifted(block, axis, distance):
    devices = range(lax.axis_size(axis))
    route = [((i - distance) % len(devices), i) for i in devices]
    return lax.ppermute(block, axis, route)


def across_rows(field):
    return (field[2:] - field[:-2]) * 0.5


def along_cols(field):
    return (jnp.roll(field, -1, -1) - jnp.roll(field, 1, -1)) * 0.5


def advance(padded, coefficients, courant):
    height = padded[0]
    eastward = padded[1]
    northward = padded[2]
    new_height = height[1:-1] - courant * coefficients[0, 1:-1] * (
        across_rows(eastward) + along_cols(northward)[1:-1]
    )
    retain = 1.0 - coefficients[1, 2:-2]
    east_middle = eastward[2:-2]
    north_middle = northward[2:-2]
    new_east = (
        retain * east_middle + courant * coriolis * north_middle - courant * across_rows(new_height)
    )
    new_north = (
        retain * north_middle
        - courant * coriolis * east_middle
        - courant * along_cols(new_height)[1:-1]
    )
    return jnp.stack((new_height[1:-1], new_east, new_north))


def body(cpoint_guess, tide_forcing, depth, drag):
    coefficients = with_halo(jnp.stack((depth, drag)), (("space", 1),), 4)
    narrow = coefficients[:, 2:-2]

    def one_substep(state, courant):
        padded = with_halo(state, (("space", 1),), 2)
        return advance(padded, narrow, courant)

    def fine_map(state):
        padded = with_halo(state, (("space", 1),), 4)
        middle = advance(padded, coefficients, fine_courant)
        result = advance(middle, narrow, fine_courant)
        return result

    def coarse_map(state):
        return one_substep(state, coarse_courant)

    def pass_on(state, stride, mapper):
        result = shifted(mapper(state), "tm", stride)
        return result

    start = cpoint_guess[0]
    state = start
    for moment in range(1, tide_forcing.shape[0]):
        state = fine_map(state) + tide_forcing[moment]
    right = pass_on(state, 1, fine_map) + tide_forcing[0] - start
    rights = [right]
    for level in range(1, LEVELS):
        current = rights[-1]
        rights.append(current + pass_on(current, 2 ** (level - 1), coarse_map))
    top_stride = 2 ** (LEVELS - 1)
    points = lax.axis_size("tm") // top_stride
    position = lax.axis_index("tm")
    base = rights[-1]
    anchor = position % top_stride == 0

    def sweep(counter, correction):
        arrived = pass_on(correction, top_stride, coarse_map)
        target = jnp.logical_and(anchor, position // top_stride == counter % points)
        return jnp.where(target, arrived + base, correction)

    correction = lax.fori_loop(1, points + 1, sweep, base)
    for level in range(LEVELS - 1, 0, -1):
        stride = 2 ** (level - 1)
        arrived = pass_on(correction, stride, coarse_map)
        odd_point = position % (2 * stride) == stride
        correction = jnp.where(odd_point, arrived + rights[level - 1], correction)
    state = start + correction
    states = [state]
    for moment in range(1, tide_forcing.shape[0]):
        state = fine_map(state) + tide_forcing[moment]
        states.append(state)
    return (jnp.stack(states), right[None])


def cycle_kernel(
    guess, forcing, depth, drag, out, residual,
    coef, track, mid, edges, edges_in, ahead, ahead_in, first, second, third, fourth,
    climb, final, final_in, residual_in, relax, wave,
    coef_sems, edge_send, edge_recv, ahead_sems, res_send, res_recv,
    first_sems, second_sems, third_sems, fourth_send, fourth_recv, relay_send,
    sibling_sems, final_sems,
):
    tm = lax.axis_index("tm")
    sp = lax.axis_index("space")
    count = lax.axis_size("tm")
    moments = forcing.shape[0]
    own = guess.shape[2]
    rows = 2 * own
    cols = guess.shape[3]
    lanes = 128
    strips = cols // lanes
    other = 1 - sp
    before = (tm + count - 1) % count
    after = (tm + 1) % count
    odd = tm % 2
    chip = (tm // 2) % 2
    layer = tm // 4
    pair = layer % 2
    half = layer // 2
    facing = tm + 2 - 4 * chip
    beside = tm + 4 - 8 * pair
    inner = pair != half
    inward = (tm + 4 - 8 * half + count) % count
    outward = (tm - 4 + 8 * half + count) % count

    def remote(src, dst, send, recv, to):
        return pltpu.make_async_remote_copy(
            src_ref=src, dst_ref=dst, send_sem=send, recv_sem=recv,
            device_id=to, device_id_type=pl.DeviceIdType.MESH,
        )

    barrier = pltpu.get_barrier_semaphore()
    partners = [
        (tm, other), (before, sp), (after, sp), (before, other), (after, other),
        (facing, sp), ((tm + 4) % count, sp), ((tm + count - 4) % count, sp),
    ]
    for to in partners:
        pl.semaphore_signal(barrier, inc=1, device_id=to, device_id_type=pl.DeviceIdType.MESH)

    lane = lax.broadcasted_iota(jnp.int32, (rows, lanes), 1)
    first_lane = lane == 0
    last_lane = lane == lanes - 1

    def strip(index):
        return pl.ds(pl.multiple_of(index * lanes, lanes), lanes)

    def down_rows(a):
        return pltpu.roll(a, rows - 1, 0) - pltpu.roll(a, 1, 0)

    def down_cols(a, following, preceding):
        return pltpu.roll(jnp.where(first_lane, following, a), lanes - 1, 1) - pltpu.roll(
            jnp.where(last_lane, preceding, a), 1, 1
        )

    def substep(src, dst, courant):
        def heights(j, carry):
            here = strip(j)
            u = src[1, :, here]
            v = src[2, :, here]
            spread = down_rows(u) + down_cols(
                v, src[2, :, strip((j + 1) % strips)], src[2, :, strip((j + strips - 1) % strips)]
            )
            dst[0, :, here] = src[0, :, here] - courant * coef[0, :, here] * spread
            return carry

        def speeds(j, carry):
            here = strip(j)
            u = src[1, :, here]
            v = src[2, :, here]
            h = dst[0, :, here]
            retain = coef[1, :, here]
            dst[1, :, here] = (
                retain * u + courant * coriolis * v - courant * 0.5 * down_rows(h)
            )
            dst[2, :, here] = (
                retain * v - courant * coriolis * u - courant * 0.5 * down_cols(
                    h, dst[0, :, strip((j + 1) % strips)],
                    dst[0, :, strip((j + strips - 1) % strips)],
                )
            )
            return carry

        lax.fori_loop(0, strips, heights, 0, unroll=True)
        lax.fori_loop(0, strips, speeds, 0, unroll=True)

    def fine(src, dst):
        substep(src, mid, fine_courant)
        substep(mid, dst, fine_courant)

    def coarse(src, dst):
        substep(src, dst, coarse_courant)

    coef[0, 0:own] = 0.5 * depth[...]
    coef[1, 0:own] = 1.0 - drag[...]
    track[0, :, 0:own] = guess[0]
    track[0, :, own:rows] = jnp.zeros((3, own, cols), jnp.float32)
    ahead[...] = forcing[0] - guess[0]
    relax[0, :, 0:own] = jnp.zeros((3, own, cols), jnp.float32)

    pl.semaphore_wait(barrier, len(partners))
    coef_copy = remote(
        coef.at[:, 0:own], coef.at[:, own:rows], coef_sems.at[0], coef_sems.at[1], (tm, other)
    )
    coef_copy.start()
    ahead_copy = remote(ahead, ahead_in, ahead_sems.at[0], ahead_sems.at[1], (before, sp))
    ahead_copy.start()

    def edge_copy(moment):
        return remote(
            edges.at[moment], edges_in.at[moment], edge_send.at[moment], edge_recv.at[moment],
            (tm, other),
        )

    upper = lax.broadcasted_iota(jnp.int32, (3, own // 2, cols), 1) < 4
    coef_copy.wait()

    def propagate(moment, carry):
        previous = moment - 1
        edges[previous] = jnp.where(
            upper, track[previous, :, 0 : own // 2], track[previous, :, own // 2 : own]
        )
        edge_copy(previous).start()
        fine(track.at[previous], track.at[moment])
        track[moment, :, 0:own] += forcing[moment]
        return carry

    lax.fori_loop(1, moments, propagate, 0)
    mine = first.at[odd]
    fine(track.at[moments - 1], mine)
    ahead_copy.wait()
    first[odd, :, 0:own] += ahead_in[...]

    first_copy = remote(first.at[0], first.at[0], first_sems.at[0], first_sems.at[1], (after, sp))

    @pl.when(odd == 0)
    def _():
        first_copy.start()

    res_here = remote(
        first.at[odd, :, 0:own], residual_in.at[0], res_send.at[0], res_recv.at[0], (after, sp)
    )
    res_there = remote(
        first.at[odd, :, own:rows], residual_in.at[1], res_send.at[1], res_recv.at[1],
        (after, other),
    )

    def relaxed(low, high):
        def step(moment, carry):
            previous = moment - 1
            edge_copy(previous).wait()
            a = previous % 2
            b = moment % 2
            relax[a, :, own : own + own // 2] = edges_in[previous]
            relax[a, :, own + own // 2 : rows] = edges_in[previous]
            fine(relax.at[a], relax.at[b])
            track[moment, :, 0:own] += relax[b, :, 0:own]
            return carry

        lax.fori_loop(low, high, step, 0)

    second_copy = remote(
        second.at[chip], second.at[chip], second_sems.at[0], second_sems.at[1], (facing, sp)
    )
    second_in = remote(
        second.at[1 - chip], second.at[1 - chip], second_sems.at[0], second_sems.at[1],
        (facing, sp),
    )
    third_copy = remote(
        third.at[pair], third.at[pair], third_sems.at[0], third_sems.at[1], (beside, sp)
    )
    third_in = remote(
        third.at[1 - pair], third.at[1 - pair], third_sems.at[0], third_sems.at[1], (beside, sp)
    )

    def gather(field, to):
        return remote(
            fourth.at[half, field], fourth.at[half, field], fourth_send.at[field],
            fourth_recv.at[field], (to, sp),
        )

    def relay(field, to):
        return remote(
            fourth.at[1 - half, field], fourth.at[1 - half, field], relay_send.at[field],
            fourth_recv.at[field], (to, sp),
        )

    @pl.when(odd == 1)
    def _():
        first_copy.wait_recv()
        coarse(first.at[0], second.at[chip])
        second[chip] += first[1]
        second_copy.start()

    res_here.start()
    res_there.start()
    relaxed(1, 3)

    @pl.when(odd == 1)
    def _():
        second_in.wait_recv()
        coarse(second.at[0], third.at[pair])
        third[pair] += second[1]
        third_copy.start()

    relaxed(3, 5)

    @pl.when(odd == 1)
    def _():
        third_in.wait_recv()
        coarse(third.at[0], fourth.at[half])
        fourth[half] += third[1]

        @pl.when(inner)
        def _():
            for field in range(3):
                gather(field, inward).start()

    relaxed(5, moments)

    @pl.when(odd == 1)
    def _():
        for field in range(3):
            relay(field, inward).wait_recv()

            @pl.when(inner)
            def _():
                relay(field, outward).start()

        coarse(fourth.at[0], climb.at[0])
        climb[0] += fourth[1]
        coarse(climb.at[0], climb.at[1])
        climb[1] += climb[0]

        def rise(take, src, dst, lower):
            @pl.when(take == 1)
            def _():
                coarse(src, dst)
                dst[...] += lower[...]

            @pl.when(take == 0)
            def _():
                dst[...] = src[...]

        rise(half, climb.at[1], climb.at[0], fourth.at[0])
        rise(pair, climb.at[0], climb.at[1], third.at[0])
        rise(chip, climb.at[1], climb.at[0], second.at[0])

    sibling = remote(climb.at[0], final, sibling_sems.at[0], sibling_sems.at[1], (before, sp))

    @pl.when(odd == 1)
    def _():
        sibling.start()
        coarse(climb.at[0], final)
        final[...] += first[0]

    @pl.when(odd == 0)
    def _():
        sibling.wait_recv()

    final_copy = remote(final, final_in, final_sems.at[0], final_sems.at[1], (tm, other))
    final_copy.start()

    res_here.wait()
    res_there.wait()
    residual[0] = residual_in[0] + residual_in[1]

    @pl.when(odd == 0)
    def _():
        first_copy.wait_send()

    @pl.when(odd == 1)
    def _():
        second_copy.wait_send()
        third_copy.wait_send()
        sibling.wait_send()

        @pl.when(inner)
        def _():
            for field in range(3):
                gather(field, inward).wait_send()
                relay(field, outward).wait_send()

    final_copy.wait()
    wave[0, :, 0:own] = final[:, 0:own] + final_in[:, own:rows]
    wave[0, :, own:rows] = final[:, own:rows] + final_in[:, 0:own]
    out[0] = guess[0] + wave[0, :, 0:own]

    def correct(moment, carry):
        a = (moment - 1) % 2
        b = moment % 2
        fine(wave.at[a], wave.at[b])
        out[moment] = track[moment, :, 0:own] + wave[b, :, 0:own]
        return carry

    lax.fori_loop(1, moments, correct, 0)


def kernel_body(cpoint_guess, tide_forcing, depth, drag):
    moments, fields, own, cols = tide_forcing.shape
    block = (fields, 2 * own, cols)
    part = (fields, own, cols)
    edge = (moments - 1, fields, own // 2, cols)

    def held(*shape):
        return pltpu.VMEM(shape, jnp.float32)

    dma = pltpu.SemaphoreType.DMA
    vmem = pl.BlockSpec(memory_space=pltpu.VMEM)
    return pl.pallas_call(
        cycle_kernel,
        out_shape=(
            jax.ShapeDtypeStruct(tide_forcing.shape, jnp.float32),
            jax.ShapeDtypeStruct(cpoint_guess.shape, jnp.float32),
        ),
        in_specs=[vmem] * 4,
        out_specs=(vmem, vmem),
        scratch_shapes=[
            held(2, 2 * own, cols),
            held(moments, *block),
            held(*block),
            held(*edge),
            held(*edge),
            held(*part),
            held(*part),
            held(2, *block),
            held(2, *block),
            held(2, *block),
            held(2, *block),
            held(2, *block),
            held(*block),
            held(*block),
            held(2, *part),
            held(2, *block),
            held(2, *block),
            dma((2,)),
            dma((moments - 1,)),
            dma((moments - 1,)),
            dma((2,)),
            dma((2,)),
            dma((2,)),
            dma((2,)),
            dma((2,)),
            dma((2,)),
            dma((3,)),
            dma((3,)),
            dma((3,)),
            dma((2,)),
            dma((2,)),
        ],
        compiler_params=pltpu.CompilerParams(
            collective_id=0, has_side_effects=True, vmem_limit_bytes=48 * 1024 * 1024
        ),
    )(cpoint_guess, tide_forcing, depth, drag)


def solution(mesh):
    placed = (
        P("tm", None, "space", None),
        P("tm", None, "space", None),
        P("space", None),
        P("space", None),
    )
    one_top_point = mesh.shape["tm"] == 2 ** (LEVELS - 1)
    fits = one_top_point and mesh.shape["space"] == 2
    return jax.shard_map(
        kernel_body if fits else body,
        mesh=mesh,
        in_specs=placed,
        out_specs=(P("tm", None, "space", None), P("tm", None, "space", None)),
        check_vma=False,
    )
```

```python
import jax
import jax.numpy as jnp
from jax import lax
from jax.experimental import pallas as pl
from jax.experimental.pallas import tpu as pltpu
from jax.sharding import PartitionSpec as P

LEVELS = 5


coriolis = 0.1
fine_courant = 0.25
coarse_courant = 0.5


def with_halo(cells, sides, width):
    for axis, dim in sides:
        count = lax.axis_size(axis)
        head = lax.slice_in_dim(cells, 0, width, axis=dim)
        tail = lax.slice_in_dim(cells, cells.shape[dim] - width, cells.shape[dim], axis=dim)
        cells = jnp.concatenate(
            [
                lax.ppermute(tail, axis, [(i, (i + 1) % count) for i in range(count)]),
                cells,
                lax.ppermute(head, axis, [((i + 1) % count, i) for i in range(count)]),
            ],
            axis=dim,
        )
    return cells


def shifted(block, axis, distance):
    devices = range(lax.axis_size(axis))
    route = [((i - distance) % len(devices), i) for i in devices]
    return lax.ppermute(block, axis, route)


def across_rows(field):
    return (field[2:] - field[:-2]) * 0.5


def along_cols(field):
    return (jnp.roll(field, -1, -1) - jnp.roll(field, 1, -1)) * 0.5


def advance(padded, coefficients, courant):
    height = padded[0]
    eastward = padded[1]
    northward = padded[2]
    new_height = height[1:-1] - courant * coefficients[0, 1:-1] * (
        across_rows(eastward) + along_cols(northward)[1:-1]
    )
    retain = 1.0 - coefficients[1, 2:-2]
    east_middle = eastward[2:-2]
    north_middle = northward[2:-2]
    new_east = (
        retain * east_middle + courant * coriolis * north_middle - courant * across_rows(new_height)
    )
    new_north = (
        retain * north_middle
        - courant * coriolis * east_middle
        - courant * along_cols(new_height)[1:-1]
    )
    return jnp.stack((new_height[1:-1], new_east, new_north))


def body(cpoint_guess, tide_forcing, depth, drag):
    coefficients = with_halo(jnp.stack((depth, drag)), (("space", 1),), 4)
    narrow = coefficients[:, 2:-2]

    def one_substep(state, courant):
        padded = with_halo(state, (("space", 1),), 2)
        return advance(padded, narrow, courant)

    def fine_map(state):
        padded = with_halo(state, (("space", 1),), 4)
        middle = advance(padded, coefficients, fine_courant)
        result = advance(middle, narrow, fine_courant)
        return result

    def coarse_map(state):
        return one_substep(state, coarse_courant)

    def pass_on(state, stride, mapper):
        result = shifted(mapper(state), "tm", stride)
        return result

    start = cpoint_guess[0]
    state = start
    for moment in range(1, tide_forcing.shape[0]):
        state = fine_map(state) + tide_forcing[moment]
    right = pass_on(state, 1, fine_map) + tide_forcing[0] - start
    rights = [right]
    for level in range(1, LEVELS):
        current = rights[-1]
        rights.append(current + pass_on(current, 2 ** (level - 1), coarse_map))
    top_stride = 2 ** (LEVELS - 1)
    points = lax.axis_size("tm") // top_stride
    position = lax.axis_index("tm")
    base = rights[-1]
    anchor = position % top_stride == 0

    def sweep(counter, correction):
        arrived = pass_on(correction, top_stride, coarse_map)
        target = jnp.logical_and(anchor, position // top_stride == counter % points)
        return jnp.where(target, arrived + base, correction)

    correction = lax.fori_loop(1, points + 1, sweep, base)
    for level in range(LEVELS - 1, 0, -1):
        stride = 2 ** (level - 1)
        arrived = pass_on(correction, stride, coarse_map)
        odd_point = position % (2 * stride) == stride
        correction = jnp.where(odd_point, arrived + rights[level - 1], correction)
    state = start + correction
    states = [state]
    for moment in range(1, tide_forcing.shape[0]):
        state = fine_map(state) + tide_forcing[moment]
        states.append(state)
    return (jnp.stack(states), right[None])


def cycle_kernel(
    guess_hbm, forcing_hbm, depth_hbm, drag_hbm, out, residual,
    guess, forcing, depth, drag, coef, track, mid, edges, edges_in, ahead, ahead_in, first, second, third, fourth,
    climb, lower_in, lower_sum, climb_in, residual_in, relax, wave,
    coef_sems, edge_send, edge_recv, ahead_sems, res_send, res_recv,
    first_sems, second_sems, third_sems, fourth_send, fourth_recv, relay_send,
    sibling_sems, climb_sems, lower_sems, load_sems,
):
    tm = lax.axis_index("tm")
    sp = lax.axis_index("space")
    count = lax.axis_size("tm")
    moments = forcing.shape[0]
    loads = [
        pltpu.make_async_copy(src, dst, load_sems.at[index])
        for index, (src, dst) in enumerate((
            (depth_hbm, depth),
            (drag_hbm, drag),
            (guess_hbm, guess),
            (forcing_hbm.at[0], forcing.at[0]),
            (forcing_hbm.at[1:moments], forcing.at[1:moments]),
        ))
    ]
    for load in loads:
        load.start()
    own = guess.shape[2]
    rows = 2 * own
    cols = guess.shape[3]
    lanes = 128
    strips = cols // lanes
    other = 1 - sp
    before = (tm + count - 1) % count
    after = (tm + 1) % count
    odd = tm % 2
    chip = (tm // 2) % 2
    layer = tm // 4
    pair = layer % 2
    half = layer // 2
    facing = tm + 2 - 4 * chip
    beside = tm + 4 - 8 * pair
    inner = pair != half
    inward = (tm + 4 - 8 * half + count) % count
    outward = (tm - 4 + 8 * half + count) % count

    def remote(src, dst, send, recv, to):
        return pltpu.make_async_remote_copy(
            src_ref=src, dst_ref=dst, send_sem=send, recv_sem=recv,
            device_id=to, device_id_type=pl.DeviceIdType.MESH,
        )

    barrier = pltpu.get_barrier_semaphore()
    partners = [
        (tm, other), (before, sp), (after, sp), (before, other), (after, other),
        (facing, sp), ((tm + 4) % count, sp), ((tm + count - 4) % count, sp),
    ]
    for to in partners:
        pl.semaphore_signal(barrier, inc=1, device_id=to, device_id_type=pl.DeviceIdType.MESH)

    lane = lax.broadcasted_iota(jnp.int32, (rows, lanes), 1)
    first_lane = lane == 0
    last_lane = lane == lanes - 1

    def strip(index):
        return pl.ds(pl.multiple_of(index * lanes, lanes), lanes)

    def down_rows(a):
        return pltpu.roll(a, rows - 1, 0) - pltpu.roll(a, 1, 0)

    def down_cols(a, following, preceding):
        return pltpu.roll(jnp.where(first_lane, following, a), lanes - 1, 1) - pltpu.roll(
            jnp.where(last_lane, preceding, a), 1, 1
        )

    def substep(src, dst, courant):
        def heights(j, carry):
            here = strip(j)
            u = src[1, :, here]
            v = src[2, :, here]
            spread = down_rows(u) + down_cols(
                v, src[2, :, strip((j + 1) % strips)], src[2, :, strip((j + strips - 1) % strips)]
            )
            dst[0, :, here] = src[0, :, here] - courant * coef[0, :, here] * spread
            return carry

        def speeds(j, carry):
            here = strip(j)
            u = src[1, :, here]
            v = src[2, :, here]
            h = dst[0, :, here]
            retain = coef[1, :, here]
            dst[1, :, here] = (
                retain * u + courant * coriolis * v - courant * 0.5 * down_rows(h)
            )
            dst[2, :, here] = (
                retain * v - courant * coriolis * u - courant * 0.5 * down_cols(
                    h, dst[0, :, strip((j + 1) % strips)],
                    dst[0, :, strip((j + strips - 1) % strips)],
                )
            )
            return carry

        lax.fori_loop(0, strips, heights, 0, unroll=True)
        lax.fori_loop(0, strips, speeds, 0, unroll=True)

    def fine(src, dst):
        substep(src, mid, fine_courant)
        substep(mid, dst, fine_courant)

    def coarse(src, dst):
        substep(src, dst, coarse_courant)

    for load in loads[:4]:
        load.wait()
    coef[0, 0:own] = 0.5 * depth[...]
    coef[1, 0:own] = 1.0 - drag[...]
    track[0, :, 0:own] = guess[0]
    track[0, :, own:rows] = jnp.zeros((3, own, cols), jnp.float32)
    ahead[...] = forcing[0] - guess[0]
    relax[0, :, 0:own] = jnp.zeros((3, own, cols), jnp.float32)

    pl.semaphore_wait(barrier, len(partners))
    coef_copy = remote(
        coef.at[:, 0:own], coef.at[:, own:rows], coef_sems.at[0], coef_sems.at[1], (tm, other)
    )
    coef_copy.start()
    ahead_copy = remote(ahead, ahead_in, ahead_sems.at[0], ahead_sems.at[1], (before, sp))
    ahead_copy.start()

    def edge_copy(moment):
        return remote(
            edges.at[moment], edges_in.at[moment], edge_send.at[moment], edge_recv.at[moment],
            (tm, other),
        )

    upper = lax.broadcasted_iota(jnp.int32, (3, own // 2, cols), 1) < 4
    loads[4].wait()
    coef_copy.wait()

    def propagate(moment, carry):
        previous = moment - 1
        edges[previous] = jnp.where(
            upper, track[previous, :, 0 : own // 2], track[previous, :, own // 2 : own]
        )
        edge_copy(previous).start()
        fine(track.at[previous], track.at[moment])
        track[moment, :, 0:own] += forcing[moment]
        return carry

    lax.fori_loop(1, moments, propagate, 0)
    mine = first.at[odd]
    fine(track.at[moments - 1], mine)
    ahead_copy.wait()
    first[odd, :, 0:own] += ahead_in[...]

    first_copy = remote(first.at[0], first.at[0], first_sems.at[0], first_sems.at[1], (after, sp))

    @pl.when(odd == 0)
    def _():
        first_copy.start()

    res_here = remote(
        first.at[odd, :, 0:own], residual_in.at[0], res_send.at[0], res_recv.at[0], (after, sp)
    )
    res_there = remote(
        first.at[odd, :, own:rows], residual_in.at[1], res_send.at[1], res_recv.at[1],
        (after, other),
    )

    def relaxed(low, high):
        def step(moment, carry):
            previous = moment - 1
            edge_copy(previous).wait()
            a = previous % 2
            b = moment % 2
            relax[a, :, own : own + own // 2] = edges_in[previous]
            relax[a, :, own + own // 2 : rows] = edges_in[previous]
            fine(relax.at[a], relax.at[b])
            track[moment, :, 0:own] += relax[b, :, 0:own]
            return carry

        lax.fori_loop(low, high, step, 0)

    lower_copy = remote(
        first.at[0], lower_in, lower_sems.at[0], lower_sems.at[1], (tm, other)
    )
    second_copy = remote(
        second.at[chip], second.at[chip], second_sems.at[0], second_sems.at[1], (facing, sp)
    )
    second_in = remote(
        second.at[1 - chip], second.at[1 - chip], second_sems.at[0], second_sems.at[1],
        (facing, sp),
    )
    third_copy = remote(
        third.at[pair], third.at[pair], third_sems.at[0], third_sems.at[1], (beside, sp)
    )
    third_in = remote(
        third.at[1 - pair], third.at[1 - pair], third_sems.at[0], third_sems.at[1], (beside, sp)
    )

    def gather(field, to):
        return remote(
            fourth.at[half, field], fourth.at[half, field], fourth_send.at[field],
            fourth_recv.at[field], (to, sp),
        )

    def relay(field, to):
        return remote(
            fourth.at[1 - half, field], fourth.at[1 - half, field], relay_send.at[field],
            fourth_recv.at[field], (to, sp),
        )

    @pl.when(odd == 1)
    def _():
        first_copy.wait_recv()
        coarse(first.at[0], second.at[chip])
        second[chip] += first[1]
        second_copy.start()
        lower_copy.start()

    res_here.start()
    res_there.start()
    relaxed(1, 3)

    @pl.when(odd == 1)
    def _():
        second_in.wait_recv()
        coarse(second.at[0], third.at[pair])
        third[pair] += second[1]
        third_copy.start()

    relaxed(3, 5)

    @pl.when(odd == 1)
    def _():
        third_in.wait_recv()
        coarse(third.at[0], fourth.at[half])
        fourth[half] += third[1]

        @pl.when(inner)
        def _():
            for field in range(3):
                gather(field, inward).start()

    relaxed(5, moments)

    @pl.when(odd == 1)
    def _():
        for field in range(3):
            relay(field, inward).wait_recv()

            @pl.when(inner)
            def _():
                relay(field, outward).start()

        coarse(fourth.at[0], climb.at[0])
        climb[0] += fourth[1]
        coarse(climb.at[0], climb.at[1])
        climb[1] += climb[0]

        def rise(take, src, dst, lower):
            @pl.when(take == 1)
            def _():
                coarse(src, dst)
                dst[...] += lower[...]

            @pl.when(take == 0)
            def _():
                dst[...] = src[...]

        rise(half, climb.at[1], climb.at[0], fourth.at[0])
        rise(pair, climb.at[0], climb.at[1], third.at[0])
        rise(chip, climb.at[1], climb.at[0], second.at[0])

    climb_copy = remote(
        climb.at[0], climb_in, climb_sems.at[0], climb_sems.at[1], (tm, other)
    )
    sibling = remote(climb.at[1], wave.at[0], sibling_sems.at[0], sibling_sems.at[1], (before, sp))

    @pl.when(odd == 1)
    def _():
        climb_copy.start()

    res_here.wait()
    res_there.wait()
    residual[0] = residual_in[0] + residual_in[1]

    @pl.when(odd == 0)
    def _():
        first_copy.wait_send()

    @pl.when(odd == 1)
    def _():
        second_copy.wait_send()
        third_copy.wait_send()
        @pl.when(inner)
        def _():
            for field in range(3):
                gather(field, inward).wait_send()
                relay(field, outward).wait_send()

    def combine(dst, kept, arrived):
        dst[:, 0:own] = kept[:, 0:own] + arrived[:, own:rows]
        dst[:, own:rows] = kept[:, own:rows] + arrived[:, 0:own]

    @pl.when(odd == 1)
    def _():
        lower_copy.wait()
        combine(lower_sum, first.at[0], lower_in)
        climb_copy.wait()
        combine(climb.at[1], climb.at[0], climb_in)
        sibling.start()
        coarse(climb.at[1], wave.at[0])
        wave[0] += lower_sum[...]
        sibling.wait_send()

    @pl.when(odd == 0)
    def _():
        sibling.wait_recv()

    out[0] = guess[0] + wave[0, :, 0:own]

    def correct(moment, carry):
        a = (moment - 1) % 2
        b = moment % 2
        fine(wave.at[a], wave.at[b])
        out[moment] = track[moment, :, 0:own] + wave[b, :, 0:own]
        return carry

    lax.fori_loop(1, moments, correct, 0)


def kernel_body(cpoint_guess, tide_forcing, depth, drag):
    moments, fields, own, cols = tide_forcing.shape
    block = (fields, 2 * own, cols)
    part = (fields, own, cols)
    edge = (moments - 1, fields, own // 2, cols)

    def held(*shape):
        return pltpu.VMEM(shape, jnp.float32)

    dma = pltpu.SemaphoreType.DMA
    vmem = pl.BlockSpec(memory_space=pltpu.VMEM)
    return pl.pallas_call(
        cycle_kernel,
        out_shape=(
            jax.ShapeDtypeStruct(tide_forcing.shape, jnp.float32),
            jax.ShapeDtypeStruct(cpoint_guess.shape, jnp.float32),
        ),
        in_specs=[pl.BlockSpec(memory_space=pl.ANY)] * 4,
        out_specs=(vmem, vmem),
        scratch_shapes=[
            held(*cpoint_guess.shape),
            held(*tide_forcing.shape),
            held(*depth.shape),
            held(*drag.shape),
            held(2, 2 * own, cols),
            held(moments, *block),
            held(*block),
            held(*edge),
            held(*edge),
            held(*part),
            held(*part),
            held(2, *block),
            held(2, *block),
            held(2, *block),
            held(2, *block),
            held(2, *block),
            held(*block),
            held(*block),
            held(*block),
            held(2, *part),
            held(2, *block),
            held(2, *block),
            dma((2,)),
            dma((moments - 1,)),
            dma((moments - 1,)),
            dma((2,)),
            dma((2,)),
            dma((2,)),
            dma((2,)),
            dma((2,)),
            dma((2,)),
            dma((3,)),
            dma((3,)),
            dma((3,)),
            dma((2,)),
            dma((2,)),
            dma((2,)),
            dma((5,)),
        ],
        compiler_params=pltpu.CompilerParams(
            collective_id=0, has_side_effects=True, vmem_limit_bytes=60 * 1024 * 1024
        ),
    )(cpoint_guess, tide_forcing, depth, drag)


def solution(mesh):
    placed = (
        P("tm", None, "space", None),
        P("tm", None, "space", None),
        P("space", None),
        P("space", None),
    )
    one_top_point = mesh.shape["tm"] == 2 ** (LEVELS - 1)
    fits = one_top_point and mesh.shape["space"] == 2
    return jax.shard_map(
        kernel_body if fits else body,
        mesh=mesh,
        in_specs=placed,
        out_specs=(P("tm", None, "space", None), P("tm", None, "space", None)),
        check_vma=False,
    )
```

```python
import jax
import jax.numpy as jnp
from jax import lax
from jax.experimental import pallas as pl
from jax.experimental.pallas import tpu as pltpu
from jax.sharding import PartitionSpec as P

LEVELS = 5


coriolis = 0.1
fine_courant = 0.25
coarse_courant = 0.5


def with_halo(cells, sides, width):
    for axis, dim in sides:
        count = lax.axis_size(axis)
        head = lax.slice_in_dim(cells, 0, width, axis=dim)
        tail = lax.slice_in_dim(cells, cells.shape[dim] - width, cells.shape[dim], axis=dim)
        cells = jnp.concatenate(
            [
                lax.ppermute(tail, axis, [(i, (i + 1) % count) for i in range(count)]),
                cells,
                lax.ppermute(head, axis, [((i + 1) % count, i) for i in range(count)]),
            ],
            axis=dim,
        )
    return cells


def shifted(block, axis, distance):
    devices = range(lax.axis_size(axis))
    route = [((i - distance) % len(devices), i) for i in devices]
    return lax.ppermute(block, axis, route)


def across_rows(field):
    return (field[2:] - field[:-2]) * 0.5


def along_cols(field):
    return (jnp.roll(field, -1, -1) - jnp.roll(field, 1, -1)) * 0.5


def advance(padded, coefficients, courant):
    height = padded[0]
    eastward = padded[1]
    northward = padded[2]
    new_height = height[1:-1] - courant * coefficients[0, 1:-1] * (
        across_rows(eastward) + along_cols(northward)[1:-1]
    )
    retain = 1.0 - coefficients[1, 2:-2]
    east_middle = eastward[2:-2]
    north_middle = northward[2:-2]
    new_east = (
        retain * east_middle + courant * coriolis * north_middle - courant * across_rows(new_height)
    )
    new_north = (
        retain * north_middle
        - courant * coriolis * east_middle
        - courant * along_cols(new_height)[1:-1]
    )
    return jnp.stack((new_height[1:-1], new_east, new_north))


def body(cpoint_guess, tide_forcing, depth, drag):
    coefficients = with_halo(jnp.stack((depth, drag)), (("space", 1),), 4)
    narrow = coefficients[:, 2:-2]

    def one_substep(state, courant):
        padded = with_halo(state, (("space", 1),), 2)
        return advance(padded, narrow, courant)

    def fine_map(state):
        padded = with_halo(state, (("space", 1),), 4)
        middle = advance(padded, coefficients, fine_courant)
        result = advance(middle, narrow, fine_courant)
        return result

    def coarse_map(state):
        return one_substep(state, coarse_courant)

    def pass_on(state, stride, mapper):
        result = shifted(mapper(state), "tm", stride)
        return result

    start = cpoint_guess[0]
    state = start
    for moment in range(1, tide_forcing.shape[0]):
        state = fine_map(state) + tide_forcing[moment]
    right = pass_on(state, 1, fine_map) + tide_forcing[0] - start
    rights = [right]
    for level in range(1, LEVELS):
        current = rights[-1]
        rights.append(current + pass_on(current, 2 ** (level - 1), coarse_map))
    top_stride = 2 ** (LEVELS - 1)
    points = lax.axis_size("tm") // top_stride
    position = lax.axis_index("tm")
    base = rights[-1]
    anchor = position % top_stride == 0

    def sweep(counter, correction):
        arrived = pass_on(correction, top_stride, coarse_map)
        target = jnp.logical_and(anchor, position // top_stride == counter % points)
        return jnp.where(target, arrived + base, correction)

    correction = lax.fori_loop(1, points + 1, sweep, base)
    for level in range(LEVELS - 1, 0, -1):
        stride = 2 ** (level - 1)
        arrived = pass_on(correction, stride, coarse_map)
        odd_point = position % (2 * stride) == stride
        correction = jnp.where(odd_point, arrived + rights[level - 1], correction)
    state = start + correction
    states = [state]
    for moment in range(1, tide_forcing.shape[0]):
        state = fine_map(state) + tide_forcing[moment]
        states.append(state)
    return (jnp.stack(states), right[None])


def cycle_kernel(
    guess_hbm, forcing_hbm, depth_hbm, drag_hbm, out, residual,
    guess, forcing, depth, drag, coef, track, mid, edges, edges_in, ahead, ahead_in, first, second, third, fourth,
    climb, lower_in, lower_sum, climb_in, residual_in, relax, wave,
    coef_sems, edge_send, edge_recv, ahead_sems, res_send, res_recv,
    first_sems, second_sems, third_sems, fourth_send, fourth_recv, relay_send,
    sibling_sems, climb_sems, lower_sems, load_sems,
):
    tm = lax.axis_index("tm")
    sp = lax.axis_index("space")
    count = lax.axis_size("tm")
    moments = forcing.shape[0]
    loads = [
        pltpu.make_async_copy(src, dst, load_sems.at[index])
        for index, (src, dst) in enumerate((
            (depth_hbm, depth),
            (drag_hbm, drag),
            (guess_hbm, guess),
            (forcing_hbm.at[0], forcing.at[0]),
            (forcing_hbm.at[1:moments], forcing.at[1:moments]),
        ))
    ]
    for load in loads:
        load.start()
    own = guess.shape[2]
    rows = 2 * own
    cols = guess.shape[3]
    lanes = 128
    strips = cols // lanes
    other = 1 - sp
    before = (tm + count - 1) % count
    after = (tm + 1) % count
    odd = tm % 2
    chip = (tm // 2) % 2
    layer = tm // 4
    pair = layer % 2
    half = layer // 2
    facing = tm + 2 - 4 * chip
    beside = tm + 4 - 8 * pair
    inner = pair != half
    inward = (tm + 4 - 8 * half + count) % count
    outward = (tm - 4 + 8 * half + count) % count

    def remote(src, dst, send, recv, to):
        return pltpu.make_async_remote_copy(
            src_ref=src, dst_ref=dst, send_sem=send, recv_sem=recv,
            device_id=to, device_id_type=pl.DeviceIdType.MESH,
        )

    barrier = pltpu.get_barrier_semaphore()
    partners = [
        (tm, other), (before, sp), (after, sp),
        (facing, sp), ((tm + 4) % count, sp), ((tm + count - 4) % count, sp),
    ]
    for to in partners:
        pl.semaphore_signal(barrier, inc=1, device_id=to, device_id_type=pl.DeviceIdType.MESH)

    lane = lax.broadcasted_iota(jnp.int32, (rows, lanes), 1)
    first_lane = lane == 0
    last_lane = lane == lanes - 1

    def strip(index):
        return pl.ds(pl.multiple_of(index * lanes, lanes), lanes)

    def down_rows(a):
        return pltpu.roll(a, rows - 1, 0) - pltpu.roll(a, 1, 0)

    def down_cols(a, following, preceding):
        return pltpu.roll(jnp.where(first_lane, following, a), lanes - 1, 1) - pltpu.roll(
            jnp.where(last_lane, preceding, a), 1, 1
        )

    def substep(src, dst, courant):
        def heights(j, carry):
            here = strip(j)
            u = src[1, :, here]
            v = src[2, :, here]
            spread = down_rows(u) + down_cols(
                v, src[2, :, strip((j + 1) % strips)], src[2, :, strip((j + strips - 1) % strips)]
            )
            dst[0, :, here] = src[0, :, here] - courant * coef[0, :, here] * spread
            return carry

        def speeds(j, carry):
            here = strip(j)
            u = src[1, :, here]
            v = src[2, :, here]
            h = dst[0, :, here]
            retain = coef[1, :, here]
            dst[1, :, here] = (
                retain * u + courant * coriolis * v - courant * 0.5 * down_rows(h)
            )
            dst[2, :, here] = (
                retain * v - courant * coriolis * u - courant * 0.5 * down_cols(
                    h, dst[0, :, strip((j + 1) % strips)],
                    dst[0, :, strip((j + strips - 1) % strips)],
                )
            )
            return carry

        lax.fori_loop(0, strips, heights, 0, unroll=True)
        lax.fori_loop(0, strips, speeds, 0, unroll=True)

    def fine(src, dst):
        substep(src, mid, fine_courant)
        substep(mid, dst, fine_courant)

    def coarse(src, dst):
        substep(src, dst, coarse_courant)

    for load in loads[:4]:
        load.wait()
    coef[0, 0:own] = 0.5 * depth[...]
    coef[1, 0:own] = 1.0 - drag[...]
    track[0, :, 0:own] = guess[0]
    track[0, :, own:rows] = jnp.zeros((3, own, cols), jnp.float32)
    ahead[...] = forcing[0] - guess[0]
    relax[0, :, 0:own] = jnp.zeros((3, own, cols), jnp.float32)

    pl.semaphore_wait(barrier, len(partners))
    coef_copy = remote(
        coef.at[:, 0:own], coef.at[:, own:rows], coef_sems.at[0], coef_sems.at[1], (tm, other)
    )
    coef_copy.start()
    ahead_copy = remote(ahead, ahead_in, ahead_sems.at[0], ahead_sems.at[1], (before, sp))
    ahead_copy.start()

    def edge_copy(moment):
        return remote(
            edges.at[moment], edges_in.at[moment], edge_send.at[moment], edge_recv.at[moment],
            (tm, other),
        )

    upper = lax.broadcasted_iota(jnp.int32, (3, own // 2, cols), 1) < 4
    loads[4].wait()
    coef_copy.wait()

    def propagate(moment, carry):
        previous = moment - 1
        edges[previous] = jnp.where(
            upper, track[previous, :, 0 : own // 2], track[previous, :, own // 2 : own]
        )
        edge_copy(previous).start()
        fine(track.at[previous], track.at[moment])
        track[moment, :, 0:own] += forcing[moment]
        return carry

    lax.fori_loop(1, moments, propagate, 0)
    mine = first.at[odd]
    fine(track.at[moments - 1], mine)
    ahead_copy.wait()
    first[odd, :, 0:own] += ahead_in[...]

    first_copy = remote(first.at[0], first.at[0], first_sems.at[0], first_sems.at[1], (after, sp))

    @pl.when(odd == 0)
    def _():
        first_copy.start()

    res_across = remote(
        first.at[odd, :, own:rows], residual_in.at[0], res_send.at[0], res_recv.at[0], (tm, other)
    )
    res_onward = remote(
        residual_in.at[1], residual_in.at[2], res_send.at[1], res_recv.at[1], (after, sp)
    )

    def relaxed(low, high):
        def step(moment, carry):
            previous = moment - 1
            edge_copy(previous).wait()
            a = previous % 2
            b = moment % 2
            relax[a, :, own : own + own // 2] = edges_in[previous]
            relax[a, :, own + own // 2 : rows] = edges_in[previous]
            fine(relax.at[a], relax.at[b])
            track[moment, :, 0:own] += relax[b, :, 0:own]
            return carry

        lax.fori_loop(low, high, step, 0)

    lower_copy = remote(
        first.at[0], lower_in, lower_sems.at[0], lower_sems.at[1], (tm, other)
    )
    second_copy = remote(
        second.at[chip], second.at[chip], second_sems.at[0], second_sems.at[1], (facing, sp)
    )
    second_in = remote(
        second.at[1 - chip], second.at[1 - chip], second_sems.at[0], second_sems.at[1],
        (facing, sp),
    )
    third_copy = remote(
        third.at[pair], third.at[pair], third_sems.at[0], third_sems.at[1], (beside, sp)
    )
    third_in = remote(
        third.at[1 - pair], third.at[1 - pair], third_sems.at[0], third_sems.at[1], (beside, sp)
    )

    def gather(field, to):
        return remote(
            fourth.at[half, field], fourth.at[half, field], fourth_send.at[field],
            fourth_recv.at[field], (to, sp),
        )

    def relay(field, to):
        return remote(
            fourth.at[1 - half, field], fourth.at[1 - half, field], relay_send.at[field],
            fourth_recv.at[field], (to, sp),
        )

    @pl.when(odd == 1)
    def _():
        first_copy.wait_recv()
        coarse(first.at[0], second.at[chip])
        second[chip] += first[1]
        second_copy.start()
        lower_copy.start()

    res_across.start()
    relaxed(1, 3)

    @pl.when(odd == 1)
    def _():
        second_in.wait_recv()
        coarse(second.at[0], third.at[pair])
        third[pair] += second[1]
        third_copy.start()

    relaxed(3, 5)

    @pl.when(odd == 1)
    def _():
        third_in.wait_recv()
        coarse(third.at[0], fourth.at[half])
        fourth[half] += third[1]

        @pl.when(inner)
        def _():
            for field in range(3):
                gather(field, inward).start()

    relaxed(5, moments)

    @pl.when(odd == 1)
    def _():
        for field in range(3):
            relay(field, inward).wait_recv()

            @pl.when(inner)
            def _():
                relay(field, outward).start()

        coarse(fourth.at[0], climb.at[0])
        climb[0] += fourth[1]
        coarse(climb.at[0], climb.at[1])
        climb[1] += climb[0]

        def rise(take, src, dst, lower):
            @pl.when(take == 1)
            def _():
                coarse(src, dst)
                dst[...] += lower[...]

            @pl.when(take == 0)
            def _():
                dst[...] = src[...]

        rise(half, climb.at[1], climb.at[0], fourth.at[0])
        rise(pair, climb.at[0], climb.at[1], third.at[0])
        rise(chip, climb.at[1], climb.at[0], second.at[0])

    climb_copy = remote(
        climb.at[0], climb_in, climb_sems.at[0], climb_sems.at[1], (tm, other)
    )
    sibling = remote(climb.at[1], wave.at[0], sibling_sems.at[0], sibling_sems.at[1], (before, sp))

    @pl.when(odd == 1)
    def _():
        climb_copy.start()

    res_across.wait()
    residual_in[1] = first[odd, :, 0:own] + residual_in[0]
    res_onward.start()

    @pl.when(odd == 0)
    def _():
        first_copy.wait_send()

    @pl.when(odd == 1)
    def _():
        second_copy.wait_send()
        third_copy.wait_send()
        @pl.when(inner)
        def _():
            for field in range(3):
                gather(field, inward).wait_send()
                relay(field, outward).wait_send()

    def combine(dst, kept, arrived):
        dst[:, 0:own] = kept[:, 0:own] + arrived[:, own:rows]
        dst[:, own:rows] = kept[:, own:rows] + arrived[:, 0:own]

    @pl.when(odd == 1)
    def _():
        lower_copy.wait()
        combine(lower_sum, first.at[0], lower_in)
        climb_copy.wait()
        combine(climb.at[1], climb.at[0], climb_in)
        sibling.start()
        coarse(climb.at[1], wave.at[0])
        wave[0] += lower_sum[...]
        sibling.wait_send()

    @pl.when(odd == 0)
    def _():
        sibling.wait_recv()

    out[0] = guess[0] + wave[0, :, 0:own]

    def correct(moment, carry):
        a = (moment - 1) % 2
        b = moment % 2
        fine(wave.at[a], wave.at[b])
        out[moment] = track[moment, :, 0:own] + wave[b, :, 0:own]
        return carry

    lax.fori_loop(1, moments, correct, 0)
    res_onward.wait()
    residual[0] = residual_in[2]


def kernel_body(cpoint_guess, tide_forcing, depth, drag):
    moments, fields, own, cols = tide_forcing.shape
    block = (fields, 2 * own, cols)
    part = (fields, own, cols)
    edge = (moments - 1, fields, own // 2, cols)

    def held(*shape):
        return pltpu.VMEM(shape, jnp.float32)

    dma = pltpu.SemaphoreType.DMA
    vmem = pl.BlockSpec(memory_space=pltpu.VMEM)
    return pl.pallas_call(
        cycle_kernel,
        out_shape=(
            jax.ShapeDtypeStruct(tide_forcing.shape, jnp.float32),
            jax.ShapeDtypeStruct(cpoint_guess.shape, jnp.float32),
        ),
        in_specs=[pl.BlockSpec(memory_space=pltpu.HBM)] * 4,
        out_specs=(vmem, vmem),
        scratch_shapes=[
            held(*cpoint_guess.shape),
            held(*tide_forcing.shape),
            held(*depth.shape),
            held(*drag.shape),
            held(2, 2 * own, cols),
            held(moments, *block),
            held(*block),
            held(*edge),
            held(*edge),
            held(*part),
            held(*part),
            held(2, *block),
            held(2, *block),
            held(2, *block),
            held(2, *block),
            held(2, *block),
            held(*block),
            held(*block),
            held(*block),
            held(3, *part),
            held(2, *block),
            held(2, *block),
            dma((2,)),
            dma((moments - 1,)),
            dma((moments - 1,)),
            dma((2,)),
            dma((2,)),
            dma((2,)),
            dma((2,)),
            dma((2,)),
            dma((2,)),
            dma((3,)),
            dma((3,)),
            dma((3,)),
            dma((2,)),
            dma((2,)),
            dma((2,)),
            dma((5,)),
        ],
        compiler_params=pltpu.CompilerParams(
            collective_id=0, has_side_effects=True, vmem_limit_bytes=40 * 1024 * 1024
        ),
    )(cpoint_guess, tide_forcing, depth, drag)


def solution(mesh):
    placed = (
        P("tm", None, "space", None),
        P("tm", None, "space", None),
        P("space", None),
        P("space", None),
    )
    one_top_point = mesh.shape["tm"] == 2 ** (LEVELS - 1)
    fits = one_top_point and mesh.shape["space"] == 2
    return jax.shard_map(
        kernel_body if fits else body,
        mesh=mesh,
        in_specs=placed,
        out_specs=(P("tm", None, "space", None), P("tm", None, "space", None)),
        check_vma=False,
    )
```

```python
import jax
import jax.numpy as jnp
from jax import lax
from jax.experimental import pallas as pl
from jax.experimental.pallas import tpu as pltpu
from jax.sharding import PartitionSpec as P

LEVELS = 5


coriolis = 0.1
fine_courant = 0.25
coarse_courant = 0.5


def with_halo(cells, sides, width):
    for axis, dim in sides:
        count = lax.axis_size(axis)
        head = lax.slice_in_dim(cells, 0, width, axis=dim)
        tail = lax.slice_in_dim(cells, cells.shape[dim] - width, cells.shape[dim], axis=dim)
        cells = jnp.concatenate(
            [
                lax.ppermute(tail, axis, [(i, (i + 1) % count) for i in range(count)]),
                cells,
                lax.ppermute(head, axis, [((i + 1) % count, i) for i in range(count)]),
            ],
            axis=dim,
        )
    return cells


def shifted(block, axis, distance):
    devices = range(lax.axis_size(axis))
    route = [((i - distance) % len(devices), i) for i in devices]
    return lax.ppermute(block, axis, route)


def across_rows(field):
    return (field[2:] - field[:-2]) * 0.5


def along_cols(field):
    return (jnp.roll(field, -1, -1) - jnp.roll(field, 1, -1)) * 0.5


def advance(padded, coefficients, courant):
    height = padded[0]
    eastward = padded[1]
    northward = padded[2]
    new_height = height[1:-1] - courant * coefficients[0, 1:-1] * (
        across_rows(eastward) + along_cols(northward)[1:-1]
    )
    retain = 1.0 - coefficients[1, 2:-2]
    east_middle = eastward[2:-2]
    north_middle = northward[2:-2]
    new_east = (
        retain * east_middle + courant * coriolis * north_middle - courant * across_rows(new_height)
    )
    new_north = (
        retain * north_middle
        - courant * coriolis * east_middle
        - courant * along_cols(new_height)[1:-1]
    )
    return jnp.stack((new_height[1:-1], new_east, new_north))


def body(cpoint_guess, tide_forcing, depth, drag):
    coefficients = with_halo(jnp.stack((depth, drag)), (("space", 1),), 4)
    narrow = coefficients[:, 2:-2]

    def one_substep(state, courant):
        padded = with_halo(state, (("space", 1),), 2)
        return advance(padded, narrow, courant)

    def fine_map(state):
        padded = with_halo(state, (("space", 1),), 4)
        middle = advance(padded, coefficients, fine_courant)
        result = advance(middle, narrow, fine_courant)
        return result

    def coarse_map(state):
        return one_substep(state, coarse_courant)

    def pass_on(state, stride, mapper):
        result = shifted(mapper(state), "tm", stride)
        return result

    start = cpoint_guess[0]
    state = start
    for moment in range(1, tide_forcing.shape[0]):
        state = fine_map(state) + tide_forcing[moment]
    right = pass_on(state, 1, fine_map) + tide_forcing[0] - start
    rights = [right]
    for level in range(1, LEVELS):
        current = rights[-1]
        rights.append(current + pass_on(current, 2 ** (level - 1), coarse_map))
    top_stride = 2 ** (LEVELS - 1)
    points = lax.axis_size("tm") // top_stride
    position = lax.axis_index("tm")
    base = rights[-1]
    anchor = position % top_stride == 0

    def sweep(counter, correction):
        arrived = pass_on(correction, top_stride, coarse_map)
        target = jnp.logical_and(anchor, position // top_stride == counter % points)
        return jnp.where(target, arrived + base, correction)

    correction = lax.fori_loop(1, points + 1, sweep, base)
    for level in range(LEVELS - 1, 0, -1):
        stride = 2 ** (level - 1)
        arrived = pass_on(correction, stride, coarse_map)
        odd_point = position % (2 * stride) == stride
        correction = jnp.where(odd_point, arrived + rights[level - 1], correction)
    state = start + correction
    states = [state]
    for moment in range(1, tide_forcing.shape[0]):
        state = fine_map(state) + tide_forcing[moment]
        states.append(state)
    return (jnp.stack(states), right[None])


def cycle_kernel(
    guess_hbm, forcing_hbm, depth_hbm, drag_hbm, out, residual,
    guess, forcing, depth, drag, coef, track, mid, edges, edges_in, ahead, ahead_in, first, second, third, fourth,
    climb, lower_in, lower_sum, climb_in, residual_in, relax, wave,
    coef_sems, edge_send, edge_recv, ahead_sems, res_send, res_recv,
    first_sems, second_sems, third_sems, fourth_send, fourth_recv, relay_send,
    sibling_sems, climb_sems, lower_sems, load_sems,
):
    tm = lax.axis_index("tm")
    sp = lax.axis_index("space")
    count = lax.axis_size("tm")
    moments = forcing.shape[0]
    loads = [
        pltpu.make_async_copy(src, dst, load_sems.at[index])
        for index, (src, dst) in enumerate((
            (depth_hbm, depth),
            (drag_hbm, drag),
            (guess_hbm, guess),
            (forcing_hbm.at[0], forcing.at[0]),
            (forcing_hbm.at[1:moments], forcing.at[1:moments]),
        ))
    ]
    for load in loads:
        load.start()
    own = guess.shape[2]
    rows = 2 * own
    cols = guess.shape[3]
    lanes = 128
    strips = cols // lanes
    other = 1 - sp
    before = (tm + count - 1) % count
    after = (tm + 1) % count
    odd = tm % 2
    chip = (tm // 2) % 2
    layer = tm // 4
    pair = layer % 2
    half = layer // 2
    facing = tm + 2 - 4 * chip
    beside = tm + 4 - 8 * pair
    inner = pair != half
    inward = (tm + 4 - 8 * half + count) % count
    outward = (tm - 4 + 8 * half + count) % count

    def remote(src, dst, send, recv, to):
        return pltpu.make_async_remote_copy(
            src_ref=src, dst_ref=dst, send_sem=send, recv_sem=recv,
            device_id=to, device_id_type=pl.DeviceIdType.MESH,
        )

    barrier = pltpu.get_barrier_semaphore()
    partners = [
        (tm, other), (before, sp), (after, sp),
        (facing, sp), ((tm + 4) % count, sp), ((tm + count - 4) % count, sp),
    ]
    for to in partners:
        pl.semaphore_signal(barrier, inc=1, device_id=to, device_id_type=pl.DeviceIdType.MESH)

    lane = lax.broadcasted_iota(jnp.int32, (rows, lanes), 1)
    first_lane = lane == 0
    last_lane = lane == lanes - 1

    def strip(index):
        return pl.ds(pl.multiple_of(index * lanes, lanes), lanes)

    def down_rows(a):
        return pltpu.roll(a, rows - 1, 0) - pltpu.roll(a, 1, 0)

    def down_cols(a, following, preceding):
        return pltpu.roll(jnp.where(first_lane, following, a), lanes - 1, 1) - pltpu.roll(
            jnp.where(last_lane, preceding, a), 1, 1
        )

    def substep(src, dst, courant):
        def heights(j, carry):
            here = strip(j)
            u = src[1, :, here]
            v = src[2, :, here]
            spread = down_rows(u) + down_cols(
                v, src[2, :, strip((j + 1) % strips)], src[2, :, strip((j + strips - 1) % strips)]
            )
            dst[0, :, here] = src[0, :, here] - courant * coef[0, :, here] * spread
            return carry

        def speeds(j, carry):
            here = strip(j)
            u = src[1, :, here]
            v = src[2, :, here]
            h = dst[0, :, here]
            retain = coef[1, :, here]
            dst[1, :, here] = (
                retain * u + courant * coriolis * v - courant * 0.5 * down_rows(h)
            )
            dst[2, :, here] = (
                retain * v - courant * coriolis * u - courant * 0.5 * down_cols(
                    h, dst[0, :, strip((j + 1) % strips)],
                    dst[0, :, strip((j + strips - 1) % strips)],
                )
            )
            return carry

        lax.fori_loop(0, strips, heights, 0, unroll=True)
        lax.fori_loop(0, strips, speeds, 0, unroll=True)

    def fine(src, dst):
        substep(src, mid, fine_courant)
        substep(mid, dst, fine_courant)

    def coarse(src, dst):
        substep(src, dst, coarse_courant)

    for load in loads[:4]:
        load.wait()
    coef[0, 0:own] = 0.5 * depth[...]
    coef[1, 0:own] = 1.0 - drag[...]
    track[0, :, 0:own] = guess[0]
    track[0, :, own:rows] = jnp.zeros((3, own, cols), jnp.float32)
    ahead[...] = forcing[0] - guess[0]
    relax[0, :, 0:own] = jnp.zeros((3, own, cols), jnp.float32)

    pl.semaphore_wait(barrier, len(partners))
    coef_copy = remote(
        coef.at[:, 0:own], coef.at[:, own:rows], coef_sems.at[0], coef_sems.at[1], (tm, other)
    )
    coef_copy.start()
    ahead_copy = remote(ahead, ahead_in, ahead_sems.at[0], ahead_sems.at[1], (before, sp))
    ahead_copy.start()

    def edge_copy(moment):
        return remote(
            edges.at[moment], edges_in.at[moment], edge_send.at[moment], edge_recv.at[moment],
            (tm, other),
        )

    upper = lax.broadcasted_iota(jnp.int32, (3, own // 2, cols), 1) < 4
    loads[4].wait()
    coef_copy.wait()

    def propagate(moment, carry):
        previous = moment - 1
        edges[previous] = jnp.where(
            upper, track[previous, :, 0 : own // 2], track[previous, :, own // 2 : own]
        )
        edge_copy(previous).start()
        fine(track.at[previous], track.at[moment])
        track[moment, :, 0:own] += forcing[moment]
        return carry

    lax.fori_loop(1, moments, propagate, 0)
    mine = first.at[odd]
    fine(track.at[moments - 1], mine)
    ahead_copy.wait()
    first[odd, :, 0:own] += ahead_in[...]

    first_copy = remote(first.at[0], first.at[0], first_sems.at[0], first_sems.at[1], (after, sp))

    @pl.when(odd == 0)
    def _():
        first_copy.start()

    res_across = remote(
        first.at[odd, :, own:rows], residual_in.at[0], res_send.at[0], res_recv.at[0], (tm, other)
    )
    res_onward = remote(
        residual_in.at[1], residual_in.at[2], res_send.at[1], res_recv.at[1], (after, sp)
    )

    def relaxed(low, high):
        def step(moment, carry):
            previous = moment - 1
            edge_copy(previous).wait()
            a = previous % 2
            b = moment % 2
            relax[a, :, own : own + own // 2] = edges_in[previous]
            relax[a, :, own + own // 2 : rows] = edges_in[previous]
            fine(relax.at[a], relax.at[b])
            track[moment, :, 0:own] += relax[b, :, 0:own]
            return carry

        lax.fori_loop(low, high, step, 0)

    lower_copy = remote(
        first.at[0], lower_in, lower_sems.at[0], lower_sems.at[1], (tm, other)
    )
    second_copy = remote(
        second.at[chip], second.at[chip], second_sems.at[0], second_sems.at[1], (facing, sp)
    )
    second_in = remote(
        second.at[1 - chip], second.at[1 - chip], second_sems.at[0], second_sems.at[1],
        (facing, sp),
    )
    third_copy = remote(
        third.at[pair], third.at[pair], third_sems.at[0], third_sems.at[1], (beside, sp)
    )
    third_in = remote(
        third.at[1 - pair], third.at[1 - pair], third_sems.at[0], third_sems.at[1], (beside, sp)
    )

    def gather(field, to):
        return remote(
            fourth.at[half, field], fourth.at[half, field], fourth_send.at[field],
            fourth_recv.at[field], (to, sp),
        )

    def relay(field, to):
        return remote(
            fourth.at[1 - half, field], fourth.at[1 - half, field], relay_send.at[field],
            fourth_recv.at[field], (to, sp),
        )

    @pl.when(odd == 1)
    def _():
        first_copy.wait_recv()
        coarse(first.at[0], second.at[chip])
        second[chip] += first[1]
        second_copy.start()
        lower_copy.start()

    res_across.start()
    relaxed(1, 3)

    @pl.when(odd == 1)
    def _():
        second_in.wait_recv()
        coarse(second.at[0], third.at[pair])
        third[pair] += second[1]
        third_copy.start()

    relaxed(3, 5)

    @pl.when(odd == 1)
    def _():
        third_in.wait_recv()
        coarse(third.at[0], fourth.at[half])
        fourth[half] += third[1]

        @pl.when(inner)
        def _():
            for field in range(3):
                gather(field, inward).start()

    relaxed(5, moments)

    @pl.when(odd == 1)
    def _():
        for field in range(3):
            relay(field, inward).wait_recv()

            @pl.when(inner)
            def _():
                relay(field, outward).start()

        coarse(fourth.at[0], climb.at[0])
        climb[0] += fourth[1]
        coarse(climb.at[0], climb.at[1])
        climb[1] += climb[0]

        def rise(take, src, dst, lower):
            @pl.when(take == 1)
            def _():
                coarse(src, dst)
                dst[...] += lower[...]

            @pl.when(take == 0)
            def _():
                dst[...] = src[...]

        rise(half, climb.at[1], climb.at[0], fourth.at[0])
        rise(pair, climb.at[0], climb.at[1], third.at[0])
        rise(chip, climb.at[1], climb.at[0], second.at[0])

    climb_copy = remote(
        climb.at[0], climb_in, climb_sems.at[0], climb_sems.at[1], (tm, other)
    )
    sibling = remote(climb.at[1], wave.at[0], sibling_sems.at[0], sibling_sems.at[1], (before, sp))

    @pl.when(odd == 1)
    def _():
        climb_copy.start()

    res_across.wait()
    residual_in[1] = first[odd, :, 0:own] + residual_in[0]
    res_onward.start()

    @pl.when(odd == 0)
    def _():
        first_copy.wait_send()

    @pl.when(odd == 1)
    def _():
        second_copy.wait_send()
        third_copy.wait_send()
        @pl.when(inner)
        def _():
            for field in range(3):
                gather(field, inward).wait_send()
                relay(field, outward).wait_send()

    def combine(dst, kept, arrived):
        dst[:, 0:own] = kept[:, 0:own] + arrived[:, own:rows]
        dst[:, own:rows] = kept[:, own:rows] + arrived[:, 0:own]

    @pl.when(odd == 1)
    def _():
        lower_copy.wait()
        combine(lower_sum, first.at[0], lower_in)
        climb_copy.wait()
        combine(climb.at[1], climb.at[0], climb_in)
        sibling.start()
        coarse(climb.at[1], wave.at[0])
        wave[0] += lower_sum[...]
        sibling.wait_send()

    @pl.when(odd == 0)
    def _():
        sibling.wait_recv()

    out[0] = guess[0] + wave[0, :, 0:own]

    def correct(moment, carry):
        a = (moment - 1) % 2
        b = moment % 2
        fine(wave.at[a], wave.at[b])
        out[moment] = track[moment, :, 0:own] + wave[b, :, 0:own]
        return carry

    lax.fori_loop(1, moments, correct, 0)
    res_onward.wait()
    residual[0] = residual_in[2]


def kernel_body(cpoint_guess, tide_forcing, depth, drag):
    moments, fields, own, cols = tide_forcing.shape
    block = (fields, 2 * own, cols)
    part = (fields, own, cols)
    edge = (moments - 1, fields, own // 2, cols)

    def held(*shape):
        return pltpu.VMEM(shape, jnp.float32)

    dma = pltpu.SemaphoreType.DMA
    vmem = pl.BlockSpec(memory_space=pltpu.VMEM)
    return pl.pallas_call(
        cycle_kernel,
        out_shape=(
            jax.ShapeDtypeStruct(tide_forcing.shape, jnp.float32),
            jax.ShapeDtypeStruct(cpoint_guess.shape, jnp.float32),
        ),
        in_specs=[pl.BlockSpec(memory_space=pltpu.HBM)] * 4,
        out_specs=(vmem, vmem),
        scratch_shapes=[
            held(*cpoint_guess.shape),
            held(*tide_forcing.shape),
            held(*depth.shape),
            held(*drag.shape),
            held(2, 2 * own, cols),
            held(moments, *block),
            held(*block),
            held(*edge),
            held(*edge),
            held(*part),
            held(*part),
            held(2, *block),
            held(2, *block),
            held(2, *block),
            held(2, *block),
            held(2, *block),
            held(*block),
            held(*block),
            held(*block),
            held(3, *part),
            held(2, *block),
            held(2, *block),
            dma((2,)),
            dma((moments - 1,)),
            dma((moments - 1,)),
            dma((2,)),
            dma((2,)),
            dma((2,)),
            dma((2,)),
            dma((2,)),
            dma((2,)),
            dma((3,)),
            dma((3,)),
            dma((3,)),
            dma((2,)),
            dma((2,)),
            dma((2,)),
            dma((5,)),
        ],
        compiler_params=pltpu.CompilerParams(
            collective_id=0, has_side_effects=True, vmem_limit_bytes=51 * 1024 * 1024
        ),
    )(cpoint_guess, tide_forcing, depth, drag)


def solution(mesh):
    placed = (
        P("tm", None, "space", None),
        P("tm", None, "space", None),
        P("space", None),
        P("space", None),
    )
    one_top_point = mesh.shape["tm"] == 2 ** (LEVELS - 1)
    fits = one_top_point and mesh.shape["space"] == 2
    return jax.shard_map(
        kernel_body if fits else body,
        mesh=mesh,
        in_specs=placed,
        out_specs=(P("tm", None, "space", None), P("tm", None, "space", None)),
        check_vma=False,
    )
```
